32 devices in a mesh: ctx: 8 (over z, x), head: 4 (over y, core).
Axes of the slice: x: 2, y: 2, z: 4, core: 2. Of those that a mesh axis runs over, the one named last changes fastest.
Arguments:
- events: bfloat16 [2048, 512], P('ctx', 'head'), may hold values from -6 to 6
- w_proj: bfloat16 [3, 512, 128], P(None, 'head'), may hold values from -0.5091169 to 0.5091169
- targets: bfloat16 [2048, 512], P('ctx', 'head'), may hold values from -6 to 6
- negatives: bfloat16 [1920, 512], P(None, 'head'), may hold values from -6 to 6
- owners: int32 [2048, 1], P('ctx'), may hold values from 0 to 7; in each aligned block of 256 rows (0 to 255, 256 to 511, ...) at most 48 rows name the same one
- item_rows: int32 [2048], P('ctx'), may hold values from 0 to 511
Outputs:
- table_grad: float32 [4096, 512], P('ctx', 'head')
The draws below stay inside these ranges and needn't reach their ends.
Inputs may be any that keep to these rules, and one draw needn't show every extreme that they name: `owners`: among the 256 events on one index of ctx (aligned blocks of 256 rows), no owner is named more than 48 times, a bound that some block reaches.
All inputs are finite; a program needn't handle non-finite values.
Results may differ from the reference program's by a relative error of at most 0.0055.
Values may be sent and summed in bfloat16 or wider, within the bound.
A program may use at most 64 MiB of HBM per device.

```python
import math
import jax
import jax.numpy as jnp
import numpy as np
from jax import lax

HS = 128
D = 512
TOK_DEV = 256
SEQ = 2048
NEG = 1920
ROWS_OWN = 512
VOCAB = 4096
CAP = 48
N_CTX = 8


def draw_events(key, part):
    key_noise, key_offset, key_pair, key_scale = jax.random.split(key, 4)
    blocks = SEQ // TOK_DEV
    groups = D // HS
    noise_part = jax.random.normal(key_noise, (SEQ, D), jnp.float32)
    offset = 0.5 * jax.random.normal(key_offset, (1, D), jnp.float32)
    paired = jax.random.randint(key_pair, (blocks,), 0, groups)
    head_scale = jnp.exp(jax.random.uniform(key_scale, (groups,), jnp.float32, math.log(0.75), math.log(1.35)))
    row_block = lax.iota(jnp.int32, SEQ) // TOK_DEV
    feature_group = lax.iota(jnp.int32, D) // HS
    marked = jnp.take(paired, row_block)[:, None] == feature_group[None, :]
    factor = jnp.where(marked, 2.0, 1.0) * jnp.take(head_scale, feature_group)[None, :]
    return jnp.clip(noise_part * factor + offset, -6.0, 6.0).astype(jnp.bfloat16)


def draw_w_proj(key, part):
    spread = 3.2 / math.sqrt(HS)
    values = spread * jnp.clip(jax.random.normal(key, (3, D, HS), jnp.float32), -1.8, 1.8)
    return values.astype(jnp.bfloat16)


def plant(drawn, own_key, smallest, top_value):
    longest = drawn.shape.index(max(drawn.shape))
    spots = []
    for shift in (0, 1):
        where = [jax.random.randint(jax.random.fold_in(own_key, axis), (), 0, length) for axis, length in enumerate(drawn.shape)]
        where[longest] = (where[longest] + shift) % drawn.shape[longest]
        spots.append(tuple(where))
    return drawn.at[spots[0]].set(smallest).at[spots[1]].set(top_value)


def block_scale(stream_key, dims, cuts, low, top_value):
    gain, own = 1.0, jax.random.fold_in(stream_key, 6)
    for axis_at, blocks in cuts:
        draws = jnp.exp(jax.random.uniform(jax.random.fold_in(own, axis_at), (blocks,), jnp.float32, low / len(cuts), top_value / len(cuts)))
        gain = gain * jnp.repeat(draws, dims[axis_at] // blocks).reshape([-1 if axis == axis_at else 1 for axis in range(len(dims))])
    return gain


def shared_out(stream_key, own, number, rows, number_of, top, most, lean):
    ranking = jax.random.permutation(stream_key, number_of)
    crowded, ordinary = shares(number_of, rows * top, most, lean, True), shares(number_of, rows * top, most, lean, False)
    places = jnp.arange(number_of)

    def named(lengths, turn):
        used = int((lengths > 0).sum())
        fixed = max(1, used // 4)
        passed = fixed + (places - fixed + turn * (used - fixed)) % max(1, number_of - fixed)
        return jnp.zeros((number_of,), jnp.int32).at[ranking[jnp.where(places < fixed, places, passed)]].set(jnp.asarray(lengths, jnp.int32))

    lengths = jnp.where(number % 4 == 0, named(crowded, number // 4), named(ordinary, number - number // 4 - 1))
    mixed = jax.random.permutation(jax.random.fold_in(own, 3), number_of)
    giver, sink = mixed[0:number_of // 2 * 2:2], mixed[1:number_of // 2 * 2:2]
    margin = jnp.minimum(lengths[giver] - 1, most - lengths[sink]) // 2
    margin = jnp.where((giver == ranking[0]) | (sink == ranking[0]) | (lengths[sink] == 0), 0, jnp.maximum(margin, 0))
    passed = jax.random.randint(jax.random.fold_in(own, 4), (number_of // 2,), 0, 1 << 20) % (margin + 1)
    lengths = lengths.at[giver].add(-passed).at[sink].add(passed)
    members = jnp.searchsorted(jnp.cumsum(lengths), jnp.arange(rows * top), side="right").astype(jnp.int32)
    grid = members.reshape(top, rows).T
    grid = grid[jax.random.permutation(jax.random.fold_in(own, 1), rows)]
    turn = jax.random.randint(jax.random.fold_in(own, 2), (rows, 1), 0, top)
    return jnp.take_along_axis(grid, (jnp.arange(top)[None, :] + turn) % top, axis=1)


def shares(amount, total, reach, lean, full):
    portions = [(1 << 20) // math.isqrt(standing ** lean) + 1 for standing in range(1, amount + 1)]
    largest = reach if full else min(reach, max(-(-total // amount), total * portions[0] // sum(portions)))
    least = 1 if total - largest >= amount - 1 else 0
    given, surplus = [largest] + [least] * (amount - 1), total - largest - least * (amount - 1)
    while surplus > 0:
        movable = [i for i in range(1, amount) if given[i] < largest] or [i for i in range(1, amount) if given[i] < reach]
        mass, remaining = sum([portions[i] for i in movable]), surplus
        for i in movable:
            addition = min(reach - given[i], max(1, remaining * portions[i] // mass), surplus)
            given[i] = given[i] + addition
            surplus = surplus - addition
    return np.array(given)


def normal_values(key, dims, scale, most, shards=(), dtype=jnp.bfloat16):
    result = jax.random.normal(key, dims, jnp.float32) * scale
    if len(shards) > 0:
        result = block_scale(key, dims, shards, -0.22, 0.18) * result
    return jnp.clip(result, min=-most, max=most).astype(dtype)


def setup_inputs(seed: int = 0) -> dict:
    key_list = jax.random.split(jax.random.key(seed), 7)
    events = draw_events(jax.random.fold_in(key_list[6], 71), 0)
    w_proj = draw_w_proj(jax.random.fold_in(key_list[6], 71), 0)
    targets = normal_values(key_list[2], (SEQ, D), 1.0, 6.0, ((0, 8), (1, 4)))
    negatives = normal_values(key_list[3], (NEG, D), 1.0, 6.0, ((1, 4),))
    owners_keys = jax.random.split(jax.random.fold_in(key_list[4], 1), SEQ // TOK_DEV)
    owners_turns = jax.random.permutation(jax.random.fold_in(key_list[4], 3), SEQ // TOK_DEV)
    owners = jax.vmap(lambda own, number: shared_out(jax.random.fold_in(key_list[4], 2), own, number, TOK_DEV, N_CTX, 1, CAP, 2))(owners_keys, owners_turns).reshape((SEQ, 1))
    item_rows = plant(jax.random.randint(key_list[5], (SEQ,), 0, ROWS_OWN), jax.random.fold_in(key_list[5], 1), 0, ROWS_OWN - 1).astype(jnp.int32)
    return dict(events=events, w_proj=w_proj, targets=targets, negatives=negatives, owners=owners, item_rows=item_rows)


highest = lax.Precision.HIGHEST

def feature_map(raw):
    return jax.nn.elu(raw) + 1.0

def feature_slope(raw):
    return jnp.where(raw > 0, 1.0, jnp.exp(raw))

def reference(events, w_proj, targets, negatives, owners, item_rows):
    heads = D // HS
    weights = w_proj.astype(jnp.float32).reshape(3, heads, HS, HS)
    blocks = events.reshape(N_CTX, TOK_DEV, heads, HS)
    line = lax.iota(jnp.int32, TOK_DEV)
    causal = (line[:, None] >= line[None, :]).astype(jnp.float32)

    def recompute(block, state, total):
        proj = jnp.einsum('thd,chde->cthe', block.astype(jnp.float32), weights, precision=highest)
        query_map = feature_map(proj[0])
        key_map = feature_map(proj[1])
        value_rows = proj[2]
        scores = jnp.einsum('the,she->hts', query_map, key_map, precision=highest) * causal
        numer = jnp.einsum('hts,shf->thf', scores, value_rows, precision=highest)
        numer = numer + jnp.einsum('the,hef->thf', query_map, state, precision=highest)
        denom = lax.optimization_barrier(jnp.sum(scores, axis=2)).T + jnp.einsum('the,he->th', query_map, total, precision=highest)
        attended = numer / denom[:, :, None]
        return (proj, query_map, key_map, value_rows, scores, attended, denom)

    def forward_step(carry, block):
        state, total = carry
        parts = recompute(block, state, total)
        key_map, value_rows = (parts[2], parts[3])
        new_state = state + jnp.einsum('the,thf->hef', key_map, value_rows, precision=highest)
        new_total = total + lax.optimization_barrier(jnp.sum(key_map, axis=0))
        return ((new_state, new_total), (parts[5], state, total))
    start = (jnp.zeros((heads, HS, HS), jnp.float32), jnp.zeros((heads, HS), jnp.float32))
    last, (attended_all, states_in, totals_in) = lax.scan(forward_step, start, blocks)
    mixed = (blocks.astype(jnp.float32) + attended_all).astype(jnp.bfloat16).reshape(N_CTX, TOK_DEV, D)
    scale = 1.0 / math.sqrt(D)

    def score_grad(pair):
        mix_block, target_block = pair
        target_f = target_block.astype(jnp.float32)
        positive = lax.optimization_barrier(jnp.sum(mix_block.astype(jnp.float32) * target_f, axis=1)) * scale
        negative = jnp.dot(mix_block, negatives.T, preferred_element_type=jnp.float32) * scale
        sigma = jax.nn.sigmoid(negative - positive[:, None])
        weight_b = (sigma / NEG).astype(jnp.bfloat16)
        coeff = lax.optimization_barrier(jnp.sum(sigma, axis=1)) / NEG
        return jnp.dot(weight_b, negatives, preferred_element_type=jnp.float32) - coeff[:, None] * target_f
    grad_mixed = lax.map(score_grad, (mixed, targets.reshape(N_CTX, TOK_DEV, D)))
    grad_mixed = grad_mixed.reshape(N_CTX, TOK_DEV, heads, HS)

    def backward_step(carry, inputs):
        adj_state, adj_total = carry
        block, grad_out, state, total = inputs
        proj, query_map, key_map, value_rows, scores, attended, denom = recompute(block, state, total)
        d_num = grad_out / denom[:, :, None]
        d_den = -lax.optimization_barrier(jnp.sum(grad_out * attended, axis=2)) / denom
        weight_mat = (jnp.einsum('thf,shf->hts', d_num, value_rows, precision=highest) + d_den.T[:, :, None]) * causal
        d_values = jnp.einsum('she,hef->shf', key_map, adj_state, precision=highest)
        d_values = d_values + jnp.einsum('hts,thf->shf', scores, d_num, precision=highest)
        d_keys = jnp.einsum('shf,hef->she', value_rows, adj_state, precision=highest) + adj_total[None]
        d_keys = d_keys + jnp.einsum('hts,the->she', weight_mat, query_map, precision=highest)
        d_query = jnp.einsum('thf,hef->the', d_num, state, precision=highest) + d_den[:, :, None] * total[None]
        d_query = d_query + jnp.einsum('hts,she->the', weight_mat, key_map, precision=highest)
        new_state = adj_state + jnp.einsum('the,thf->hef', query_map, d_num, precision=highest)
        new_total = adj_total + jnp.einsum('th,the->he', d_den, query_map, precision=highest)
        d_raw = jnp.stack([d_query * feature_slope(proj[0]), d_keys * feature_slope(proj[1]), d_values])
        d_events = grad_out + jnp.einsum('cthe,chde->thd', d_raw, weights, precision=highest)
        return ((new_state, new_total), d_events.reshape(TOK_DEV, D))
    start_adj = (jnp.zeros((heads, HS, HS), jnp.float32), jnp.zeros((heads, HS), jnp.float32))
    final, grad_events = lax.scan(backward_step, start_adj, (blocks, grad_mixed, states_in, totals_in), reverse=True)
    grad_b = grad_events.reshape(SEQ, D).astype(jnp.bfloat16)
    target_index = owners[:, 0].astype(jnp.int32) * ROWS_OWN + item_rows.astype(jnp.int32)
    table_grad = jnp.zeros((VOCAB, D), jnp.float32).at[target_index].add(grad_b.astype(jnp.float32))
    return table_grad
```

```python
import functools
import math

import jax
import jax.numpy as jnp
from jax import lax
from jax.experimental import pallas as pl
from jax.experimental.pallas import tpu as pltpu
from jax.sharding import PartitionSpec as P

ROWS_OWN = 512
MESH = pl.DeviceIdType.MESH
F32 = jnp.float32
BF = jnp.bfloat16


def split_ctx(n):
    inner = 1
    while n % (inner * 2) == 0 and inner * inner * 4 <= n:
        inner *= 2
    return n // inner, inner


def mm(a, b, ca=1, cb=0):
    return lax.dot_general(
        a.astype(BF), b.astype(BF), (((ca,), (cb,)), ((), ())), preferred_element_type=F32
    )


def times(n, step):
    if n <= 16:
        for k in range(1, n):
            step(k)
    else:

        @pl.loop(1, n)
        def _(k):
            step(k)


def kernel(
    n_ctx, n_head, capacity, pieces,
    ev_ref, w_ref, tg_ref, neg_hbm, own_ref, item_ref,
    out_ref,
    negs, mixes, poss, ids_send, ids_recv, rows_send, rows_recv,
    state_own, state_in, state_mid, state_mid_in,
    adj_own, adj_in, adj_mid, adj_mid_in,
    acc, sums,
    sem_local, sem_ids, sem_neg, sem_fwd, sem_mix, sem_pos,
    sem_st, sem_st2, sem_ad, sem_ad2, sem_rows,
):
    outer, inner = split_ctx(n_ctx)
    length, size = ev_ref.shape
    neg_count = neg_hbm.shape[0]
    scale = 1.0 / math.sqrt(size * n_head)
    pairs = n_head // 2
    me = lax.axis_index("ctx")
    a, b = me // inner, me % inner
    h = lax.axis_index("head")
    p, c = h // 2, h % 2
    mate = p * 2 + (1 - c)

    barrier = pltpu.get_barrier_semaphore()

    def greet_ctx(k):
        pl.semaphore_signal(
            barrier, inc=1, device_id={"ctx": (me + k) % n_ctx}, device_id_type=MESH
        )

    def greet_head(k):
        pl.semaphore_signal(
            barrier, inc=1, device_id={"head": (h + k) % n_head}, device_id_type=MESH
        )

    times(n_ctx, greet_ctx)
    times(n_head, greet_head)

    def remote(src, dst, send, recv, **where):
        return pltpu.make_async_remote_copy(
            src_ref=src, dst_ref=dst, send_sem=send, recv_sem=recv,
            device_id=where, device_id_type=MESH,
        )

    local_neg = pltpu.make_async_copy(neg_hbm, negs.at[h], sem_local)
    local_neg.start()

    ev = ev_ref[...]
    raw_k = mm(ev, w_ref[1])
    val = mm(ev, w_ref[2])
    slope_k = jnp.exp(jnp.minimum(raw_k, 0.0))
    km = slope_k + jnp.maximum(raw_k, 0.0)
    own_rows = state_own.shape[0]
    line_pad = lax.broadcasted_iota(jnp.int32, (own_rows - size, size), 0)

    def pack(mat, row):
        tail = jnp.where(line_pad == 0, jnp.broadcast_to(row, line_pad.shape), 0.0)
        return jnp.concatenate([mat, tail], axis=0)

    own_state = pack(mm(km, val, 0, 0), jnp.sum(km, axis=0, keepdims=True))
    state_own[...] = own_state.astype(BF)

    pl.semaphore_wait(barrier, n_ctx - 1 + n_head - 1)

    def outer_copy(own, slots, sem, k, forward):
        to = a + k if forward else a - k
        return remote(own, slots.at[k], sem.at[0, k], sem.at[1, k], ctx=to * inner + b)

    def outer_there(k, forward):
        return a + k < outer if forward else a - k >= 0

    def outer_start(own, slots, sem, forward):
        def step(k):
            @pl.when(outer_there(k, forward))
            def _():
                outer_copy(own, slots, sem, k, forward).start()

        times(outer, step)

    def outer_sum(own, slots, sem, forward):
        acc[...] = jnp.zeros_like(acc)

        def step(k):
            @pl.when(outer_there(k, not forward))
            def _():
                outer_copy(own, slots, sem, k, not forward).wait_recv()
                acc[...] += slots[k].astype(F32)

        times(outer, step)

    def outer_end(own, slots, sem, forward):
        def step(k):
            @pl.when(outer_there(k, forward))
            def _():
                outer_copy(own, slots, sem, k, forward).wait_send()

        times(outer, step)

    def inner_copy(mids, slots, sem, j):
        to = a * inner + (b + j) % inner
        return remote(mids.at[j], slots.at[j], sem.at[0, j], sem.at[1, j], ctx=to)

    def inner_start(own_value, mids, slots, sem, forward):
        def step(j):
            to = (b + j) % inner
            passed = b < to if forward else b > to
            mids[j] = (acc[...] + jnp.where(passed, own_value, 0.0)).astype(BF)
            inner_copy(mids, slots, sem, j).start()

        times(inner, step)

    def inner_sum(mids, slots, sem):
        def step(j):
            inner_copy(mids, slots, sem, j).wait()
            acc[...] += slots[j].astype(F32)

        times(inner, step)

    outer_start(state_own, state_in, sem_st, True)

    piece = neg_count // pieces

    def neg_copy(slot, i, to, send, recv, source=None):
        rows = pl.ds(i * piece, piece)
        src = negs.at[slot, rows] if source is None else source.at[rows]
        return remote(src, negs.at[slot, rows], send, recv, head=to)

    def neg_far(i, k):
        to = ((p + k) % pairs) * 2 + c
        return neg_copy(h, i, to, sem_neg.at[0, k, i], sem_neg.at[1, k, i], neg_hbm)

    def neg_near(i):
        return neg_copy(h, i, mate, sem_neg.at[0, 0, i], sem_neg.at[1, 0, i], neg_hbm)

    def neg_from_far(i, k):
        slot = ((p - k + pairs) % pairs) * 2 + c
        return neg_copy(slot, i, mate, sem_neg.at[0, k, i], sem_neg.at[1, k, i])

    def neg_pass(i, k):
        slot = ((p - k + pairs) % pairs) * 2 + c
        return neg_copy(slot, i, mate, sem_fwd.at[0, k, i], sem_fwd.at[1, k, i])

    for i in range(pieces):
        for k in range(1, pairs):
            neg_far(i, k).start()
    for i in range(pieces):
        neg_near(i).start()

    raw_q = mm(ev, w_ref[0])
    slope_q = jnp.exp(jnp.minimum(raw_q, 0.0))
    qm = slope_q + jnp.maximum(raw_q, 0.0)
    at_row = lax.broadcasted_iota(jnp.int32, (length, length), 0)
    at_col = lax.broadcasted_iota(jnp.int32, (length, length), 1)
    causal = at_row >= at_col
    scores = jnp.where(causal, mm(qm, km, 1, 1), 0.0)
    scores_b = scores.astype(BF)
    numer = mm(scores_b, val)
    denom = jnp.sum(scores, axis=1, keepdims=True)

    outer_sum(state_own, state_in, sem_st, True)
    inner_start(own_state, state_mid, state_mid_in, sem_st2, True)

    lanes = ids_send.shape[2]
    hot = own_ref[...] == lax.broadcasted_iota(jnp.int32, (length, lanes), 1)
    hot_f = hot.astype(F32)
    earlier = mm((at_row > at_col).astype(F32), hot_f)
    rank = jnp.sum(earlier * hot_f, axis=1, keepdims=True).astype(jnp.int32)
    rank_hot = (rank == lax.broadcasted_iota(jnp.int32, (length, lanes), 1)).astype(F32)
    number = item_ref[...] + 1
    hot_t = hot_f.T
    high = mm(hot_t * (number // 16).astype(F32), rank_hot)
    low = mm(hot_t * (number % 16).astype(F32), rank_hot)
    numbers = (high * 16.0 + low).astype(jnp.int32)
    for d in range(n_ctx):
        ids_send[d] = numbers[d : d + 1, :]

    def ids_copy(k):
        to = (me + k) % n_ctx
        return remote(
            ids_send.at[to], ids_recv.at[me], sem_ids.at[0, k], sem_ids.at[1, k], ctx=to
        )

    def ids_from(k):
        at = (me - k + n_ctx) % n_ctx
        return remote(
            ids_send.at[at], ids_recv.at[at], sem_ids.at[0, k], sem_ids.at[1, k], ctx=at
        )

    times(n_ctx, lambda k: ids_copy(k).start())
    ids_recv[me] = ids_send[me]
    slot = own_ref[...] * capacity + rank
    placing = (
        slot == lax.broadcasted_iota(jnp.int32, (length, n_ctx * capacity), 1)
    ).astype(F32).astype(BF)

    inner_sum(state_mid, state_mid_in, sem_st2)
    state = acc[0:size, :]
    total = acc[size : size + 1, :]
    state_b = state.astype(BF)

    numer = numer + mm(qm, state_b)
    denom = denom + jnp.sum(qm * total, axis=1, keepdims=True)
    inverse = 1.0 / denom
    att = numer * inverse
    mixed = (ev.astype(F32) + att).astype(BF)
    mixes[h] = mixed

    def mix_copy(k):
        to = (h + k) % n_head
        return remote(mixes.at[h], mixes.at[h], sem_mix.at[0, k], sem_mix.at[1, k], head=to)

    def mix_from(k):
        at = (h - k + n_head) % n_head
        return remote(mixes.at[at], mixes.at[at], sem_mix.at[0, k], sem_mix.at[1, k], head=at)

    def pos_copy(k):
        to = (h + k) % n_head
        return remote(poss.at[h], poss.at[h], sem_pos.at[0, k], sem_pos.at[1, k], head=to)

    def pos_from(k):
        at = (h - k + n_head) % n_head
        return remote(poss.at[at], poss.at[at], sem_pos.at[0, k], sem_pos.at[1, k], head=at)

    for k in range(1, n_head):
        mix_copy(k).start()
    targets = tg_ref[...].astype(F32)
    pos = jnp.sum(mixed.astype(F32) * targets, axis=1, keepdims=True)
    poss[h] = jnp.broadcast_to(pos, (length, size)).T[0:8, :]
    for k in range(1, n_head):
        pos_copy(k).start()

    for i in range(pieces):
        for k in range(1, pairs):
            neg_from_far(i, k).wait_recv()
            neg_pass(i, k).start()
    for k in range(1, n_head):
        mix_from(k).wait_recv()
        pos_from(k).wait_recv()
    local_neg.wait()

    pos_all = poss[0]
    for k in range(1, n_head):
        pos_all = pos_all + poss[k]
    pos_col = pos_all.T[:, 0:1] * (0.5 * scale)
    mixed_all = jnp.concatenate([mixes[k] for k in range(n_head)], axis=1)

    grad = jnp.zeros((length, size), F32)
    coef = jnp.zeros((length, 1), F32)
    for i in range(pieces):
        rows = pl.ds(i * piece, piece)
        neg_near(i).wait_recv()
        for k in range(1, pairs):
            neg_pass(i, k).wait_recv()
        block = jnp.concatenate([negs[k, rows] for k in range(n_head)], axis=1)
        score = mm(mixed_all, block, 1, 1)
        sigma = 0.5 + 0.5 * jnp.tanh(score * (0.5 * scale) - pos_col)
        coef = coef + jnp.sum(sigma, axis=1, keepdims=True)
        grad = grad + mm((sigma * (1.0 / neg_count)).astype(BF), negs[h, rows])
    grad = grad - (coef * (1.0 / neg_count)) * targets

    d_num = grad * inverse
    d_den = -jnp.sum(grad * att, axis=1, keepdims=True) * inverse
    d_num_b = d_num.astype(BF)
    qm_b = qm.astype(BF)
    own_adj = pack(mm(qm_b, d_num_b, 0, 0), jnp.sum(d_den * qm, axis=0, keepdims=True))
    adj_own[...] = own_adj.astype(BF)
    outer_start(adj_own, adj_in, sem_ad, False)

    weight = jnp.where(causal, mm(d_num_b, val, 1, 1) + d_den, 0.0).astype(BF)
    d_val = mm(scores_b, d_num_b, 0, 0)
    d_key = mm(weight, qm_b, 0, 0)
    d_query = mm(d_num_b, state_b, 1, 1) + d_den * total + mm(weight, km)
    grad = grad + mm(d_query * slope_q, w_ref[0], 1, 1)

    outer_sum(adj_own, adj_in, sem_ad, False)
    inner_start(own_adj, adj_mid, adj_mid_in, sem_ad2, False)

    times(n_ctx, lambda k: ids_from(k).wait_recv())
    numbers = jnp.concatenate([ids_recv[s][:, 0:capacity] for s in range(n_ctx)], axis=1)
    picking = (
        numbers - 1
        == lax.broadcasted_iota(jnp.int32, (ROWS_OWN, n_ctx * capacity), 0)
    ).astype(F32).astype(BF)

    inner_sum(adj_mid, adj_mid_in, sem_ad2)
    adj = acc[0:size, :].astype(BF)
    adj_total = acc[size : size + 1, :]
    d_val = d_val + mm(km, adj)
    d_key = d_key + mm(val, adj, 1, 1) + adj_total
    grad = grad + mm(d_key * slope_k, w_ref[1], 1, 1) + mm(d_val, w_ref[2], 1, 1)
    placed = mm(placing, grad.astype(BF), 0, 0).astype(BF)
    rows_send[...] = placed.reshape(n_ctx, capacity, size)

    def rows_copy(k):
        to = (me + k) % n_ctx
        return remote(
            rows_send.at[to], rows_recv.at[me], sem_rows.at[0, k], sem_rows.at[1, k], ctx=to
        )

    def rows_from(k):
        at = (me - k + n_ctx) % n_ctx
        return remote(
            rows_send.at[at], rows_recv.at[at], sem_rows.at[0, k], sem_rows.at[1, k], ctx=at
        )

    times(n_ctx, lambda k: rows_copy(k).start())
    rows_recv[me] = rows_send[me]

    outer_end(state_own, state_in, sem_st, True)
    outer_end(adj_own, adj_in, sem_ad, False)
    times(n_ctx, lambda k: ids_copy(k).wait_send())
    for k in range(1, n_head):
        mix_copy(k).wait_send()
        pos_copy(k).wait_send()
    for i in range(pieces):
        neg_near(i).wait_send()
        for k in range(1, pairs):
            neg_far(i, k).wait_send()
            neg_pass(i, k).wait_send()
    times(n_ctx, lambda k: rows_copy(k).wait_send())
    times(n_ctx, lambda k: rows_from(k).wait_recv())
    out_ref[...] = mm(picking, rows_recv[...].reshape(n_ctx * capacity, size))


def body(n_ctx, n_head, events, w_proj, targets, negatives, owners, item_rows):
    length, size = events.shape
    neg_count = negatives.shape[0]
    capacity = -(-(3 * length // (2 * n_ctx)) // 16) * 16
    outer, inner = split_ctx(n_ctx)
    pieces = 3
    packed = size + 16
    lanes = max(128, n_ctx)
    dma = pltpu.SemaphoreType.DMA
    vmem = pl.BlockSpec(memory_space=pltpu.VMEM)
    scans = [
        pltpu.VMEM((packed, size), BF),
        pltpu.VMEM((outer, packed, size), BF),
        pltpu.VMEM((max(inner, 2), packed, size), BF),
        pltpu.VMEM((max(inner, 2), packed, size), BF),
    ]
    return pl.pallas_call(
        functools.partial(kernel, n_ctx, n_head, capacity, pieces),
        out_shape=jax.ShapeDtypeStruct((ROWS_OWN, size), F32),
        in_specs=[vmem, vmem, vmem, pl.BlockSpec(memory_space=pl.ANY), vmem, vmem],
        out_specs=vmem,
        scratch_shapes=[
            pltpu.VMEM((n_head, neg_count, size), BF),
            pltpu.VMEM((n_head, length, size), BF),
            pltpu.VMEM((n_head, 8, length), F32),
            pltpu.VMEM((n_ctx, 1, lanes), jnp.int32),
            pltpu.VMEM((n_ctx, 1, lanes), jnp.int32),
            pltpu.VMEM((n_ctx, capacity, size), BF),
            pltpu.VMEM((n_ctx, capacity, size), BF),
            *scans,
            *scans,
            pltpu.VMEM((packed, size), F32),
            pltpu.VMEM((8, 128), F32),
            dma,
            dma((2, n_ctx)),
            dma((2, n_head // 2, pieces)),
            dma((2, n_head // 2, pieces)),
            dma((2, n_head)),
            dma((2, n_head)),
            dma((2, outer)),
            dma((2, max(inner, 2))),
            dma((2, outer)),
            dma((2, max(inner, 2))),
            dma((2, n_ctx)),
        ],
        compiler_params=pltpu.CompilerParams(
            collective_id=0, has_side_effects=True, vmem_limit_bytes=48 * 1024 * 1024
        ),
    )(events, w_proj, targets, negatives, owners, item_rows.reshape(1, length))


def solution(mesh):
    placed = (
        P("ctx", "head"),
        P(None, "head", None),
        P("ctx", "head"),
        P(None, "head"),
        P("ctx", None),
        P("ctx"),
    )
    return jax.shard_map(
        functools.partial(body, mesh.shape["ctx"], mesh.shape["head"]),
        mesh=mesh, in_specs=placed, out_specs=P("ctx", "head"), check_vma=False,
    )
```

```python
import functools
import math

import jax
import jax.numpy as jnp
from jax import lax
from jax.experimental import pallas as pl
from jax.experimental.pallas import tpu as pltpu
from jax.sharding import PartitionSpec as P

ROWS_OWN = 512
MESH = pl.DeviceIdType.MESH
F32 = jnp.float32
BF = jnp.bfloat16


def split_ctx(n):
    inner = 1
    while n % (inner * 2) == 0 and inner * inner * 2 <= n:
        inner *= 2
    return n // inner, inner


def mm(a, b, ca=1, cb=0):
    return lax.dot_general(
        a.astype(BF), b.astype(BF), (((ca,), (cb,)), ((), ())), preferred_element_type=F32
    )


def times(n, step):
    if n <= 16:
        for k in range(1, n):
            step(k)
    else:

        @pl.loop(1, n)
        def _(k):
            step(k)


def kernel(
    n_ctx, n_head, capacity, pieces,
    ev_hbm, w_hbm, tg_hbm, neg_hbm, own_hbm, item_hbm,
    out_ref,
    ev_ref, w_ref, tg_ref, own_ref, item_ref,
    negs, mixes, poss, ids_send, ids_recv, rows_send, rows_recv,
    state_own, state_in, state_mid, state_mid_in,
    adj_own, adj_in, adj_mid, adj_mid_in,
    acc,
    sem_local, sem_ids, sem_near, sem_far, sem_cross, sem_pass, sem_mix, sem_pos,
    sem_st, sem_st2, sem_ad, sem_ad2, sem_rows,
):
    outer, inner = split_ctx(n_ctx)
    length, size = ev_hbm.shape
    neg_count = neg_hbm.shape[0]
    scale = 1.0 / math.sqrt(size * n_head)
    pairs = n_head // 2
    me = lax.axis_index("ctx")
    a, b = me // inner, me % inner
    h = lax.axis_index("head")
    p, c = h // 2, h % 2
    mate = p * 2 + (1 - c)

    barrier = pltpu.get_barrier_semaphore()

    def greet_ctx(k):
        pl.semaphore_signal(
            barrier, inc=1, device_id={"ctx": (me + k) % n_ctx}, device_id_type=MESH
        )

    def greet_head(k):
        pl.semaphore_signal(
            barrier, inc=1, device_id={"head": (h + k) % n_head}, device_id_type=MESH
        )

    times(n_ctx, greet_ctx)
    times(n_head, greet_head)

    def remote(src, dst, send, recv, **where):
        return pltpu.make_async_remote_copy(
            src_ref=src, dst_ref=dst, send_sem=send, recv_sem=recv,
            device_id=where, device_id_type=MESH,
        )

    loads = [
        pltpu.make_async_copy(src, dst, sem_local.at[i])
        for i, (src, dst) in enumerate(
            (
                (ev_hbm, ev_ref),
                (w_hbm, w_ref),
                (own_hbm, own_ref),
                (item_hbm, item_ref),
                (tg_hbm, tg_ref),
                (neg_hbm, negs.at[h]),
            )
        )
    ]
    for load in loads:
        load.start()
    loads[0].wait()
    loads[1].wait()

    ev = ev_ref[...]
    raw_k = mm(ev, w_ref[1])
    val = mm(ev, w_ref[2])
    slope_k = jnp.exp(jnp.minimum(raw_k, 0.0))
    km = slope_k + jnp.maximum(raw_k, 0.0)
    own_rows = state_own.shape[0]
    line_pad = lax.broadcasted_iota(jnp.int32, (own_rows - size, size), 0)

    def pack(mat, row):
        tail = jnp.where(line_pad == 0, jnp.broadcast_to(row, line_pad.shape), 0.0)
        return jnp.concatenate([mat, tail], axis=0)

    own_state = pack(mm(km, val, 0, 0), jnp.sum(km, axis=0, keepdims=True))
    state_own[...] = own_state.astype(BF)

    pl.semaphore_wait(barrier, n_ctx - 1 + n_head - 1)

    def outer_copy(own, slots, sem, k, forward):
        to = a + k if forward else a - k
        return remote(own, slots.at[k], sem.at[0, k], sem.at[1, k], ctx=to * inner + b)

    def outer_there(k, forward):
        return a + k < outer if forward else a - k >= 0

    def outer_start(own, slots, sem, forward):
        def step(k):
            @pl.when(outer_there(k, forward))
            def _():
                outer_copy(own, slots, sem, k, forward).start()

        times(outer, step)

    def outer_sum(own, slots, sem, forward):
        acc[...] = jnp.zeros_like(acc)

        def step(k):
            @pl.when(outer_there(k, not forward))
            def _():
                outer_copy(own, slots, sem, k, not forward).wait_recv()
                acc[...] += slots[k].astype(F32)

        times(outer, step)

    def outer_end(own, slots, sem, forward):
        def step(k):
            @pl.when(outer_there(k, forward))
            def _():
                outer_copy(own, slots, sem, k, forward).wait_send()

        times(outer, step)

    def inner_copy(mids, slots, sem, j):
        to = a * inner + (b + j) % inner
        return remote(mids.at[j], slots.at[j], sem.at[0, j], sem.at[1, j], ctx=to)

    def inner_start(own_value, mids, slots, sem, forward):
        def step(j):
            to = (b + j) % inner
            passed = b < to if forward else b > to
            mids[j] = (acc[...] + jnp.where(passed, own_value, 0.0)).astype(BF)
            inner_copy(mids, slots, sem, j).start()

        times(inner, step)

    def inner_sum(mids, slots, sem):
        def step(j):
            inner_copy(mids, slots, sem, j).wait()
            acc[...] += slots[j].astype(F32)

        times(inner, step)

    outer_start(state_own, state_in, sem_st, True)

    parts = 2
    piece = neg_count // (2 * parts)
    half = me % 2
    partner = me + 1 - 2 * half

    def neg_rows(which, r):
        return pl.ds(pl.multiple_of((which * parts + r) * piece, 16), piece)

    def neg_slot(k):
        return ((p - k + pairs) % pairs) * 2 + c

    def neg_near():
        return remote(neg_hbm, negs.at[h], sem_near.at[0], sem_near.at[1], head=mate)

    def neg_far(k, r):
        rows = neg_rows(half, r)
        to = ((p + k) % pairs) * 2 + c
        return remote(
            neg_hbm.at[rows], negs.at[h, rows],
            sem_far.at[0, k, r], sem_far.at[1, k, r], head=to,
        )

    def neg_from_far(k, r):
        block = negs.at[neg_slot(k), neg_rows(half, r)]
        return remote(block, block, sem_far.at[0, k, r], sem_far.at[1, k, r], head=neg_slot(k))

    def neg_cross(k, r):
        block = negs.at[neg_slot(k), neg_rows(half, r)]
        return remote(block, block, sem_cross.at[0, k, r], sem_cross.at[1, k, r], ctx=partner)

    def neg_from_cross(k, r):
        block = negs.at[neg_slot(k), neg_rows(1 - half, r)]
        return remote(block, block, sem_cross.at[0, k, r], sem_cross.at[1, k, r], ctx=partner)

    def neg_pass(k, r, turn):
        block = negs.at[neg_slot(k), neg_rows(half if turn == 0 else 1 - half, r)]
        return remote(
            block, block, sem_pass.at[0, k, r, turn], sem_pass.at[1, k, r, turn], head=mate
        )

    def neg_forward(r):
        for k in range(1, pairs):
            neg_from_far(k, r).wait_recv()
            neg_cross(k, r).start()
            neg_pass(k, r, 0).start()

    def neg_forward_cross(r):
        for k in range(1, pairs):
            neg_from_cross(k, r).wait_recv()
            neg_pass(k, r, 1).start()

    for r in range(parts):
        for k in range(1, pairs):
            neg_far(k, r).start()
    neg_near().start()

    raw_q = mm(ev, w_ref[0])
    slope_q = jnp.exp(jnp.minimum(raw_q, 0.0))
    qm = slope_q + jnp.maximum(raw_q, 0.0)
    at_row = lax.broadcasted_iota(jnp.int32, (length, length), 0)
    at_col = lax.broadcasted_iota(jnp.int32, (length, length), 1)
    causal = at_row >= at_col
    scores = jnp.where(causal, mm(qm, km, 1, 1), 0.0)
    scores_b = scores.astype(BF)
    numer = mm(scores_b, val)
    denom = jnp.sum(scores, axis=1, keepdims=True)

    outer_sum(state_own, state_in, sem_st, True)
    inner_start(own_state, state_mid, state_mid_in, sem_st2, True)

    lanes = ids_send.shape[2]
    loads[2].wait()
    loads[3].wait()
    owner_row = own_ref[...]
    hot = (owner_row == lax.broadcasted_iota(jnp.int32, (lanes, length), 0)).astype(F32)
    earlier = mm(hot, (at_row < at_col).astype(F32))
    rank = jnp.sum(earlier * hot, axis=0, keepdims=True).astype(jnp.int32)
    rank_hot = (rank == lax.broadcasted_iota(jnp.int32, (lanes, length), 0)).astype(F32)
    number = item_ref[...] + 1
    high = mm(hot * (number // 16).astype(F32), rank_hot, 1, 1)
    low = mm(hot * (number % 16).astype(F32), rank_hot, 1, 1)
    numbers = (high * 16.0 + low).astype(jnp.int32)
    for d in range(n_ctx):
        ids_send[d] = numbers[d : d + 1, :]

    def ids_copy(k):
        to = (me + k) % n_ctx
        return remote(
            ids_send.at[to], ids_recv.at[me], sem_ids.at[0, k], sem_ids.at[1, k], ctx=to
        )

    def ids_from(k):
        at = (me - k + n_ctx) % n_ctx
        return remote(
            ids_send.at[at], ids_recv.at[at], sem_ids.at[0, k], sem_ids.at[1, k], ctx=at
        )

    times(n_ctx, lambda k: ids_copy(k).start())
    ids_recv[me] = ids_send[me]
    slot = owner_row * capacity + rank
    placing = (
        slot == lax.broadcasted_iota(jnp.int32, (n_ctx * capacity, length), 0)
    ).astype(F32).astype(BF)

    neg_forward(0)
    inner_sum(state_mid, state_mid_in, sem_st2)
    state = acc[0:size, :]
    total = acc[size : size + 1, :]
    state_b = state.astype(BF)

    numer = numer + mm(qm, state_b)
    denom = denom + jnp.sum(qm * total, axis=1, keepdims=True)
    inverse = 1.0 / denom
    att = numer * inverse
    mixed = (ev.astype(F32) + att).astype(BF)
    mixes[h] = mixed

    def mix_copy(k):
        to = (h + k) % n_head
        return remote(mixes.at[h], mixes.at[h], sem_mix.at[0, k], sem_mix.at[1, k], head=to)

    def mix_from(k):
        at = (h - k + n_head) % n_head
        return remote(mixes.at[at], mixes.at[at], sem_mix.at[0, k], sem_mix.at[1, k], head=at)

    def pos_copy(k):
        to = (h + k) % n_head
        return remote(poss.at[h], poss.at[h], sem_pos.at[0, k], sem_pos.at[1, k], head=to)

    def pos_from(k):
        at = (h - k + n_head) % n_head
        return remote(poss.at[at], poss.at[at], sem_pos.at[0, k], sem_pos.at[1, k], head=at)

    for k in range(1, n_head):
        mix_copy(k).start()
    loads[4].wait()
    targets = tg_ref[...].astype(F32)
    pos = jnp.sum(mixed.astype(F32) * targets, axis=1, keepdims=True)
    poss[h] = jnp.broadcast_to(pos, (length, size)).T[0:8, :]
    for k in range(1, n_head):
        pos_copy(k).start()

    for r in range(1, parts):
        neg_forward(r)
    for r in range(parts):
        neg_forward_cross(r)
    for k in range(1, n_head):
        mix_from(k).wait_recv()
        pos_from(k).wait_recv()
    loads[5].wait()
    neg_near().wait_recv()
    for k in range(1, pairs):
        for r in range(parts):
            neg_pass(k, r, 0).wait_recv()
            neg_pass(k, r, 1).wait_recv()

    pos_all = poss[0]
    for k in range(1, n_head):
        pos_all = pos_all + poss[k]
    pos_col = pos_all.T[:, 0:1] * (0.5 * scale)
    mixed_all = jnp.concatenate([mixes[k] for k in range(n_head)], axis=1)

    grad = jnp.zeros((length, size), F32)
    coef = jnp.zeros((length, 1), F32)
    for i in range(pieces):
        rows = pl.ds(i * (neg_count // pieces), neg_count // pieces)
        block = jnp.concatenate([negs[k, rows] for k in range(n_head)], axis=1)
        score = mm(mixed_all, block, 1, 1)
        sigma = 0.5 + 0.5 * jnp.tanh(score * (0.5 * scale) - pos_col)
        coef = coef + jnp.sum(sigma, axis=1, keepdims=True)
        grad = grad + mm((sigma * (1.0 / neg_count)).astype(BF), negs[h, rows])
    grad = grad - (coef * (1.0 / neg_count)) * targets

    d_num = grad * inverse
    d_den = -jnp.sum(grad * att, axis=1, keepdims=True) * inverse
    d_num_b = d_num.astype(BF)
    qm_b = qm.astype(BF)
    own_adj = pack(mm(qm_b, d_num_b, 0, 0), jnp.sum(d_den * qm, axis=0, keepdims=True))
    adj_own[...] = own_adj.astype(BF)
    outer_start(adj_own, adj_in, sem_ad, False)

    weight = jnp.where(causal, mm(d_num_b, val, 1, 1) + d_den, 0.0).astype(BF)
    d_val = mm(scores_b, d_num_b, 0, 0)
    d_key = mm(weight, qm_b, 0, 0)
    d_query = mm(d_num_b, state_b, 1, 1) + d_den * total + mm(weight, km)
    grad = grad + mm(d_query * slope_q, w_ref[0], 1, 1)

    outer_sum(adj_own, adj_in, sem_ad, False)
    inner_start(own_adj, adj_mid, adj_mid_in, sem_ad2, False)

    times(n_ctx, lambda k: ids_from(k).wait_recv())
    numbers = jnp.concatenate([ids_recv[s][:, 0:capacity] for s in range(n_ctx)], axis=1)
    picking = (
        numbers - 1
        == lax.broadcasted_iota(jnp.int32, (ROWS_OWN, n_ctx * capacity), 0)
    ).astype(F32).astype(BF)

    inner_sum(adj_mid, adj_mid_in, sem_ad2)
    adj = acc[0:size, :].astype(BF)
    adj_total = acc[size : size + 1, :]
    d_val = d_val + mm(km, adj)
    d_key = d_key + mm(val, adj, 1, 1) + adj_total
    grad = grad + mm(d_key * slope_k, w_ref[1], 1, 1) + mm(d_val, w_ref[2], 1, 1)
    placed = mm(placing, grad.astype(BF)).astype(BF)
    rows_send[...] = placed.reshape(n_ctx, capacity, size)

    def rows_copy(k):
        to = (me + k) % n_ctx
        return remote(
            rows_send.at[to], rows_recv.at[me], sem_rows.at[0, k], sem_rows.at[1, k], ctx=to
        )

    def rows_from(k):
        at = (me - k + n_ctx) % n_ctx
        return remote(
            rows_send.at[at], rows_recv.at[at], sem_rows.at[0, k], sem_rows.at[1, k], ctx=at
        )

    times(n_ctx, lambda k: rows_copy(k).start())
    rows_recv[me] = rows_send[me]

    outer_end(state_own, state_in, sem_st, True)
    outer_end(adj_own, adj_in, sem_ad, False)
    times(n_ctx, lambda k: ids_copy(k).wait_send())
    for k in range(1, n_head):
        mix_copy(k).wait_send()
        pos_copy(k).wait_send()
    neg_near().wait_send()
    for k in range(1, pairs):
        for r in range(parts):
            neg_far(k, r).wait_send()
            neg_cross(k, r).wait_send()
            neg_pass(k, r, 0).wait_send()
            neg_pass(k, r, 1).wait_send()
    times(n_ctx, lambda k: rows_copy(k).wait_send())
    times(n_ctx, lambda k: rows_from(k).wait_recv())
    out_ref[...] = mm(picking, rows_recv[...].reshape(n_ctx * capacity, size))


def body(n_ctx, n_head, events, w_proj, targets, negatives, owners, item_rows):
    length, size = events.shape
    neg_count = negatives.shape[0]
    capacity = -(-(3 * length // (2 * n_ctx)) // 16) * 16
    outer, inner = split_ctx(n_ctx)
    pieces = 3
    packed = size + 16
    lanes = max(128, n_ctx)
    dma = pltpu.SemaphoreType.DMA
    vmem = pl.BlockSpec(memory_space=pltpu.VMEM)
    scans = [
        pltpu.VMEM((packed, size), BF),
        pltpu.VMEM((outer, packed, size), BF),
        pltpu.VMEM((max(inner, 2), packed, size), BF),
        pltpu.VMEM((max(inner, 2), packed, size), BF),
    ]
    return pl.pallas_call(
        functools.partial(kernel, n_ctx, n_head, capacity, pieces),
        out_shape=jax.ShapeDtypeStruct((ROWS_OWN, size), F32),
        in_specs=[pl.BlockSpec(memory_space=pltpu.HBM)] * 6,
        out_specs=vmem,
        scratch_shapes=[
            pltpu.VMEM((length, size), BF),
            pltpu.VMEM(w_proj.shape, BF),
            pltpu.VMEM((length, size), BF),
            pltpu.VMEM((1, length), jnp.int32),
            pltpu.VMEM((1, length), jnp.int32),
            pltpu.VMEM((n_head, neg_count, size), BF),
            pltpu.VMEM((n_head, length, size), BF),
            pltpu.VMEM((n_head, 8, length), F32),
            pltpu.VMEM((n_ctx, 1, lanes), jnp.int32),
            pltpu.VMEM((n_ctx, 1, lanes), jnp.int32),
            pltpu.VMEM((n_ctx, capacity, size), BF),
            pltpu.VMEM((n_ctx, capacity, size), BF),
            *scans,
            *scans,
            pltpu.VMEM((packed, size), F32),
            dma((6,)),
            dma((2, n_ctx)),
            dma((2,)),
            dma((2, n_head // 2, 2)),
            dma((2, n_head // 2, 2)),
            dma((2, n_head // 2, 2, 2)),
            dma((2, n_head)),
            dma((2, n_head)),
            dma((2, outer)),
            dma((2, max(inner, 2))),
            dma((2, outer)),
            dma((2, max(inner, 2))),
            dma((2, n_ctx)),
        ],
        compiler_params=pltpu.CompilerParams(
            collective_id=0, has_side_effects=True, vmem_limit_bytes=56 * 1024 * 1024
        ),
    )(
        events,
        w_proj,
        targets,
        negatives,
        owners.reshape(1, length),
        item_rows.reshape(1, length),
    )


def solution(mesh):
    placed = (
        P("ctx", "head"),
        P(None, "head", None),
        P("ctx", "head"),
        P(None, "head"),
        P("ctx", None),
        P("ctx"),
    )
    return jax.shard_map(
        functools.partial(body, mesh.shape["ctx"], mesh.shape["head"]),
        mesh=mesh, in_specs=placed, out_specs=P("ctx", "head"), check_vma=False,
    )
```

```python
import functools
import math

import jax
import jax.numpy as jnp
from jax import lax
from jax.experimental import pallas as pl
from jax.experimental.pallas import tpu as pltpu
from jax.sharding import PartitionSpec as P

ROWS_OWN = 512
MESH = pl.DeviceIdType.MESH
F32 = jnp.float32
BF = jnp.bfloat16


def split_ctx(n):
    inner = 1
    while n % (inner * 2) == 0 and inner * inner * 2 <= n:
        inner *= 2
    return n // inner, inner


def mm(a, b, ca=1, cb=0):
    return lax.dot_general(
        a.astype(BF), b.astype(BF), (((ca,), (cb,)), ((), ())), preferred_element_type=F32
    )


def times(n, step):
    if n <= 16:
        for k in range(1, n):
            step(k)
    else:

        @pl.loop(1, n)
        def _(k):
            step(k)


def kernel(
    n_ctx, n_head, capacity, pieces,
    ev_hbm, w_hbm, tg_hbm, neg_hbm, own_hbm, item_hbm,
    rows_out, numbers_out,
    ev_ref, w_ref, tg_ref, own_ref, item_ref,
    negs, mixes, poss, ids_send, ids_recv, rows_send, rows_recv,
    state_own, state_in, state_mid, state_mid_in,
    adj_own, adj_in, adj_mid, adj_mid_in,
    acc,
    sem_local, sem_ids, sem_near, sem_far, sem_cross, sem_pass, sem_mix, sem_pos,
    sem_st, sem_st2, sem_ad, sem_ad2, sem_rows,
):
    outer, inner = split_ctx(n_ctx)
    length, size = ev_hbm.shape
    neg_count = neg_hbm.shape[0]
    scale = 1.0 / math.sqrt(size * n_head)
    pairs = n_head // 2
    me = lax.axis_index("ctx")
    a, b = me // inner, me % inner
    h = lax.axis_index("head")
    p, c = h // 2, h % 2
    mate = p * 2 + (1 - c)

    barrier = pltpu.get_barrier_semaphore()

    def greet_ctx(k):
        pl.semaphore_signal(
            barrier, inc=1, device_id={"ctx": (me + k) % n_ctx}, device_id_type=MESH
        )

    def greet_head(k):
        pl.semaphore_signal(
            barrier, inc=1, device_id={"head": (h + k) % n_head}, device_id_type=MESH
        )

    times(n_ctx, greet_ctx)
    times(n_head, greet_head)

    def remote(src, dst, send, recv, **where):
        return pltpu.make_async_remote_copy(
            src_ref=src, dst_ref=dst, send_sem=send, recv_sem=recv,
            device_id=where, device_id_type=MESH,
        )

    loads = [
        pltpu.make_async_copy(src, dst, sem_local.at[i])
        for i, (src, dst) in enumerate(
            (
                (ev_hbm, ev_ref),
                (w_hbm, w_ref),
                (own_hbm, own_ref),
                (item_hbm, item_ref),
                (tg_hbm, tg_ref),
                (neg_hbm, negs.at[h]),
            )
        )
    ]
    for load in loads:
        load.start()
    loads[0].wait()
    loads[1].wait()

    ev = ev_ref[...]
    raw_k = mm(ev, w_ref[1])
    val = mm(ev, w_ref[2])
    slope_k = jnp.exp(jnp.minimum(raw_k, 0.0))
    km = slope_k + jnp.maximum(raw_k, 0.0)
    own_rows = state_own.shape[0]
    line_pad = lax.broadcasted_iota(jnp.int32, (own_rows - size, size), 0)

    def pack(mat, row):
        tail = jnp.where(line_pad == 0, jnp.broadcast_to(row, line_pad.shape), 0.0)
        return jnp.concatenate([mat, tail], axis=0)

    own_state = pack(mm(km, val, 0, 0), jnp.sum(km, axis=0, keepdims=True))
    state_own[...] = own_state.astype(BF)

    pl.semaphore_wait(barrier, n_ctx - 1 + n_head - 1)

    chunks = (pl.ds(0, 64), pl.ds(64, own_rows - 64))

    def outer_copy(own, slots, sem, k, r, forward):
        to = a + k if forward else a - k
        rows = chunks[r]
        return remote(
            own.at[rows], slots.at[k, rows], sem.at[0, k, r], sem.at[1, k, r],
            ctx=to * inner + b,
        )

    def outer_there(k, forward):
        return a + k < outer if forward else a - k >= 0

    def outer_start(own, slots, sem, forward):
        for r in range(len(chunks)):

            def step(k):
                @pl.when(outer_there(k, forward))
                def _():
                    outer_copy(own, slots, sem, k, r, forward).start()

            times(outer, step)

    def outer_sum(own, slots, sem, r, forward):
        rows = chunks[r]
        acc[rows] = jnp.zeros((rows.size, size), F32)

        def step(k):
            @pl.when(outer_there(k, not forward))
            def _():
                outer_copy(own, slots, sem, k, r, not forward).wait_recv()
                acc[rows] += slots[k, rows].astype(F32)

        times(outer, step)

    def outer_end(own, slots, sem, forward):
        for r in range(len(chunks)):

            def step(k):
                @pl.when(outer_there(k, forward))
                def _():
                    outer_copy(own, slots, sem, k, r, forward).wait_send()

            times(outer, step)

    def inner_copy(mids, slots, sem, j, r):
        to = a * inner + (b + j) % inner
        rows = chunks[r]
        return remote(
            mids.at[j, rows], slots.at[j, rows], sem.at[0, j, r], sem.at[1, j, r], ctx=to
        )

    def inner_start(own_value, mids, slots, sem, r, forward):
        rows = chunks[r]
        mine = own_value[rows.start : rows.start + rows.size]

        def step(j):
            to = (b + j) % inner
            passed = b < to if forward else b > to
            mids[j, rows] = (acc[rows] + jnp.where(passed, mine, 0.0)).astype(BF)
            inner_copy(mids, slots, sem, j, r).start()

        times(inner, step)

    def inner_sum(mids, slots, sem):
        for r in range(len(chunks)):
            rows = chunks[r]

            def step(j):
                inner_copy(mids, slots, sem, j, r).wait()
                acc[rows] += slots[j, rows].astype(F32)

            times(inner, step)

    def scan_turn(own_value, own, slots, sem, mids, mid_slots, mid_sem, forward):
        for r in range(len(chunks)):
            outer_sum(own, slots, sem, r, forward)
            inner_start(own_value, mids, mid_slots, mid_sem, r, forward)

    outer_start(state_own, state_in, sem_st, True)

    parts = 2
    piece = neg_count // (2 * parts)
    half = me % 2
    partner = me + 1 - 2 * half

    def neg_rows(which, r):
        return pl.ds(pl.multiple_of((which * parts + r) * piece, 16), piece)

    def neg_slot(k):
        return ((p - k + pairs) % pairs) * 2 + c

    def neg_near():
        return remote(neg_hbm, negs.at[h], sem_near.at[0], sem_near.at[1], head=mate)

    def neg_far(k, r):
        rows = neg_rows(half, r)
        to = ((p + k) % pairs) * 2 + c
        return remote(
            neg_hbm.at[rows], negs.at[h, rows],
            sem_far.at[0, k, r], sem_far.at[1, k, r], head=to,
        )

    def neg_from_far(k, r):
        block = negs.at[neg_slot(k), neg_rows(half, r)]
        return remote(block, block, sem_far.at[0, k, r], sem_far.at[1, k, r], head=neg_slot(k))

    def neg_cross(k, r):
        block = negs.at[neg_slot(k), neg_rows(half, r)]
        return remote(block, block, sem_cross.at[0, k, r], sem_cross.at[1, k, r], ctx=partner)

    def neg_from_cross(k, r):
        block = negs.at[neg_slot(k), neg_rows(1 - half, r)]
        return remote(block, block, sem_cross.at[0, k, r], sem_cross.at[1, k, r], ctx=partner)

    def neg_pass(k, r, turn):
        block = negs.at[neg_slot(k), neg_rows(half if turn == 0 else 1 - half, r)]
        return remote(
            block, block, sem_pass.at[0, k, r, turn], sem_pass.at[1, k, r, turn], head=mate
        )

    def neg_forward(r):
        for k in range(1, pairs):
            neg_from_far(k, r).wait_recv()
            neg_cross(k, r).start()
            neg_pass(k, r, 0).start()

    def neg_forward_cross(r):
        for k in range(1, pairs):
            neg_from_cross(k, r).wait_recv()
            neg_pass(k, r, 1).start()

    for r in range(parts):
        for k in range(1, pairs):
            neg_far(k, r).start()
    neg_near().start()

    raw_q = mm(ev, w_ref[0])
    slope_q = jnp.exp(jnp.minimum(raw_q, 0.0))
    qm = slope_q + jnp.maximum(raw_q, 0.0)
    at_row = lax.broadcasted_iota(jnp.int32, (length, length), 0)
    at_col = lax.broadcasted_iota(jnp.int32, (length, length), 1)
    causal = at_row >= at_col
    scores = jnp.where(causal, mm(qm, km, 1, 1), 0.0)
    scores_b = scores.astype(BF)
    numer = mm(scores_b, val)
    denom = jnp.sum(scores, axis=1, keepdims=True)

    scan_turn(own_state, state_own, state_in, sem_st, state_mid, state_mid_in, sem_st2, True)

    lanes = ids_send.shape[2]
    loads[2].wait()
    loads[3].wait()
    owner_row = own_ref[...]
    hot = (owner_row == lax.broadcasted_iota(jnp.int32, (lanes, length), 0)).astype(F32)
    earlier = mm(hot, (at_row < at_col).astype(F32))
    rank = jnp.sum(earlier * hot, axis=0, keepdims=True).astype(jnp.int32)
    rank_hot = (rank == lax.broadcasted_iota(jnp.int32, (lanes, length), 0)).astype(F32)
    number = item_ref[...] + 1
    high = mm(hot * (number // 16).astype(F32), rank_hot, 1, 1)
    low = mm(hot * (number % 16).astype(F32), rank_hot, 1, 1)
    numbers = (high * 16.0 + low).astype(jnp.int32)
    for d in range(n_ctx):
        ids_send[d] = numbers[d : d + 1, :]

    def ids_copy(k):
        to = (me + k) % n_ctx
        return remote(
            ids_send.at[to], ids_recv.at[me], sem_ids.at[0, k], sem_ids.at[1, k], ctx=to
        )

    def ids_from(k):
        at = (me - k + n_ctx) % n_ctx
        return remote(
            ids_send.at[at], ids_recv.at[at], sem_ids.at[0, k], sem_ids.at[1, k], ctx=at
        )

    times(n_ctx, lambda k: ids_copy(k).start())
    ids_recv[me] = ids_send[me]
    slot = owner_row * capacity + rank
    placing = (
        slot == lax.broadcasted_iota(jnp.int32, (n_ctx * capacity, length), 0)
    ).astype(F32).astype(BF)

    neg_forward(0)
    inner_sum(state_mid, state_mid_in, sem_st2)
    state = acc[0:size, :]
    total = acc[size : size + 1, :]
    state_b = state.astype(BF)

    numer = numer + mm(qm, state_b)
    denom = denom + jnp.sum(qm * total, axis=1, keepdims=True)
    inverse = 1.0 / denom
    att = numer * inverse
    mixed = (ev.astype(F32) + att).astype(BF)
    mixes[h] = mixed

    def mix_copy(k):
        to = (h + k) % n_head
        return remote(mixes.at[h], mixes.at[h], sem_mix.at[0, k], sem_mix.at[1, k], head=to)

    def mix_from(k):
        at = (h - k + n_head) % n_head
        return remote(mixes.at[at], mixes.at[at], sem_mix.at[0, k], sem_mix.at[1, k], head=at)

    def pos_copy(k):
        to = (h + k) % n_head
        return remote(poss.at[h], poss.at[h], sem_pos.at[0, k], sem_pos.at[1, k], head=to)

    def pos_from(k):
        at = (h - k + n_head) % n_head
        return remote(poss.at[at], poss.at[at], sem_pos.at[0, k], sem_pos.at[1, k], head=at)

    for k in range(1, n_head):
        mix_copy(k).start()
    loads[4].wait()
    targets = tg_ref[...].astype(F32)
    pos = jnp.sum(mixed.astype(F32) * targets, axis=1, keepdims=True)
    poss[h] = jnp.broadcast_to(pos, (length, size)).T[0:8, :]
    for k in range(1, n_head):
        pos_copy(k).start()

    for r in range(1, parts):
        neg_forward(r)
    for r in range(parts):
        neg_forward_cross(r)
    for k in range(1, n_head):
        mix_from(k).wait_recv()
        pos_from(k).wait_recv()
    loads[5].wait()
    neg_near().wait_recv()
    for k in range(1, pairs):
        for r in range(parts):
            neg_pass(k, r, 0).wait_recv()
            neg_pass(k, r, 1).wait_recv()

    pos_all = poss[0]
    for k in range(1, n_head):
        pos_all = pos_all + poss[k]
    pos_col = pos_all.T[:, 0:1] * (0.5 * scale)
    mixed_all = jnp.concatenate([mixes[k] for k in range(n_head)], axis=1)

    grad = jnp.zeros((length, size), F32)
    coef = jnp.zeros((length, 1), F32)
    for i in range(pieces):
        rows = pl.ds(i * (neg_count // pieces), neg_count // pieces)
        block = jnp.concatenate([negs[k, rows] for k in range(n_head)], axis=1)
        score = mm(mixed_all, block, 1, 1)
        sigma = 0.5 + 0.5 * jnp.tanh(score * (0.5 * scale) - pos_col)
        coef = coef + jnp.sum(sigma, axis=1, keepdims=True)
        grad = grad + mm((sigma * (1.0 / neg_count)).astype(BF), negs[h, rows])
    grad = grad - (coef * (1.0 / neg_count)) * targets

    d_num = grad * inverse
    d_den = -jnp.sum(grad * att, axis=1, keepdims=True) * inverse
    d_num_b = d_num.astype(BF)
    qm_b = qm.astype(BF)
    own_adj = pack(mm(qm_b, d_num_b, 0, 0), jnp.sum(d_den * qm, axis=0, keepdims=True))
    adj_own[...] = own_adj.astype(BF)
    outer_start(adj_own, adj_in, sem_ad, False)

    weight = jnp.where(causal, mm(d_num_b, val, 1, 1) + d_den, 0.0).astype(BF)
    d_val = mm(scores_b, d_num_b, 0, 0)
    d_key = mm(weight, qm_b, 0, 0)
    d_query = mm(d_num_b, state_b, 1, 1) + d_den * total + mm(weight, km)
    grad = grad + mm(d_query * slope_q, w_ref[0], 1, 1)

    scan_turn(own_adj, adj_own, adj_in, sem_ad, adj_mid, adj_mid_in, sem_ad2, False)

    times(n_ctx, lambda k: ids_from(k).wait_recv())
    numbers = jnp.concatenate([ids_recv[s][:, 0:capacity] for s in range(n_ctx)], axis=1)
    numbers_out[...] = numbers

    inner_sum(adj_mid, adj_mid_in, sem_ad2)
    adj = acc[0:size, :].astype(BF)
    adj_total = acc[size : size + 1, :]
    d_val = d_val + mm(km, adj)
    d_key = d_key + mm(val, adj, 1, 1) + adj_total
    grad = grad + mm(d_key * slope_k, w_ref[1], 1, 1) + mm(d_val, w_ref[2], 1, 1)
    placed = mm(placing, grad.astype(BF)).astype(BF)
    rows_send[...] = placed.reshape(n_ctx, capacity, size)

    def rows_copy(k):
        to = (me + k) % n_ctx
        return remote(
            rows_send.at[to], rows_recv.at[me], sem_rows.at[0, k], sem_rows.at[1, k], ctx=to
        )

    def rows_from(k):
        at = (me - k + n_ctx) % n_ctx
        return remote(
            rows_send.at[at], rows_recv.at[at], sem_rows.at[0, k], sem_rows.at[1, k], ctx=at
        )

    times(n_ctx, lambda k: rows_copy(k).start())
    rows_recv[me] = rows_send[me]

    outer_end(state_own, state_in, sem_st, True)
    outer_end(adj_own, adj_in, sem_ad, False)
    times(n_ctx, lambda k: ids_copy(k).wait_send())
    for k in range(1, n_head):
        mix_copy(k).wait_send()
        pos_copy(k).wait_send()
    neg_near().wait_send()
    for k in range(1, pairs):
        for r in range(parts):
            neg_far(k, r).wait_send()
            neg_cross(k, r).wait_send()
            neg_pass(k, r, 0).wait_send()
            neg_pass(k, r, 1).wait_send()
    times(n_ctx, lambda k: rows_copy(k).wait_send())
    times(n_ctx, lambda k: rows_from(k).wait_recv())
    rows_out[...] = rows_recv[...].reshape(n_ctx * capacity, size)


def place_rows(rows_ref, numbers_ref, out_ref):
    count = out_ref.shape[0]
    first = pl.program_id(0) * count + 1
    line = lax.broadcasted_iota(jnp.int32, (count, rows_ref.shape[0]), 0) + first
    picking = (numbers_ref[...] == line).astype(F32).astype(BF)
    out_ref[...] = mm(picking, rows_ref[...])


def body(n_ctx, n_head, events, w_proj, targets, negatives, owners, item_rows):
    length, size = events.shape
    neg_count = negatives.shape[0]
    capacity = -(-(3 * length // (2 * n_ctx)) // 16) * 16
    outer, inner = split_ctx(n_ctx)
    pieces = 3
    packed = size + 16
    lanes = max(128, n_ctx)
    dma = pltpu.SemaphoreType.DMA
    vmem = pl.BlockSpec(memory_space=pltpu.VMEM)
    scans = [
        pltpu.VMEM((packed, size), BF),
        pltpu.VMEM((outer, packed, size), BF),
        pltpu.VMEM((max(inner, 2), packed, size), BF),
        pltpu.VMEM((max(inner, 2), packed, size), BF),
    ]
    rows, numbers = pl.pallas_call(
        functools.partial(kernel, n_ctx, n_head, capacity, pieces),
        out_shape=(
            jax.ShapeDtypeStruct((n_ctx * capacity, size), BF),
            jax.ShapeDtypeStruct((1, n_ctx * capacity), jnp.int32),
        ),
        in_specs=[pl.BlockSpec(memory_space=pltpu.HBM)] * 6,
        out_specs=(vmem, vmem),
        scratch_shapes=[
            pltpu.VMEM((length, size), BF),
            pltpu.VMEM(w_proj.shape, BF),
            pltpu.VMEM((length, size), BF),
            pltpu.VMEM((1, length), jnp.int32),
            pltpu.VMEM((1, length), jnp.int32),
            pltpu.VMEM((n_head, neg_count, size), BF),
            pltpu.VMEM((n_head, length, size), BF),
            pltpu.VMEM((n_head, 8, length), F32),
            pltpu.VMEM((n_ctx, 1, lanes), jnp.int32),
            pltpu.VMEM((n_ctx, 1, lanes), jnp.int32),
            pltpu.VMEM((n_ctx, capacity, size), BF),
            pltpu.VMEM((n_ctx, capacity, size), BF),
            *scans,
            *scans,
            pltpu.VMEM((packed, size), F32),
            dma((6,)),
            dma((2, n_ctx)),
            dma((2,)),
            dma((2, n_head // 2, 2)),
            dma((2, n_head // 2, 2)),
            dma((2, n_head // 2, 2, 2)),
            dma((2, n_head)),
            dma((2, n_head)),
            dma((2, outer, 2)),
            dma((2, max(inner, 2), 2)),
            dma((2, outer, 2)),
            dma((2, max(inner, 2), 2)),
            dma((2, n_ctx)),
        ],
        compiler_params=pltpu.CompilerParams(
            collective_id=0, has_side_effects=True, vmem_limit_bytes=56 * 1024 * 1024
        ),
    )(
        events,
        w_proj,
        targets,
        negatives,
        owners.reshape(1, length),
        item_rows.reshape(1, length),
    )
    blocks = 1
    return pl.pallas_call(
        place_rows,
        grid=(blocks,),
        out_shape=jax.ShapeDtypeStruct((ROWS_OWN, size), F32),
        in_specs=[
            pl.BlockSpec((n_ctx * capacity, size), lambda i: (0, 0)),
            pl.BlockSpec((1, n_ctx * capacity), lambda i: (0, 0)),
        ],
        out_specs=pl.BlockSpec((ROWS_OWN // blocks, size), lambda i: (i, 0)),
        compiler_params=pltpu.CompilerParams(vmem_limit_bytes=56 * 1024 * 1024),
    )(rows, numbers)


def solution(mesh):
    placed = (
        P("ctx", "head"),
        P(None, "head", None),
        P("ctx", "head"),
        P(None, "head"),
        P("ctx", None),
        P("ctx"),
    )
    return jax.shard_map(
        functools.partial(body, mesh.shape["ctx"], mesh.shape["head"]),
        mesh=mesh, in_specs=placed, out_specs=P("ctx", "head"), check_vma=False,
    )
```

```python
import functools
import math

import jax
import jax.numpy as jnp
from jax import lax
from jax.experimental import pallas as pl
from jax.experimental.pallas import tpu as pltpu
from jax.sharding import PartitionSpec as P

ROWS_OWN = 512
MESH = pl.DeviceIdType.MESH
F32 = jnp.float32
BF = jnp.bfloat16


def split_ctx(n):
    inner = 1
    while n % (inner * 2) == 0 and inner * inner * 2 <= n:
        inner *= 2
    return n // inner, inner


def mm(a, b, ca=1, cb=0):
    return lax.dot_general(
        a.astype(BF), b.astype(BF), (((ca,), (cb,)), ((), ())), preferred_element_type=F32
    )


def times(n, step):
    if n <= 16:
        for k in range(1, n):
            step(k)
    else:

        @pl.loop(1, n)
        def _(k):
            step(k)


def kernel(
    n_ctx, n_head, capacity, pieces,
    ev_hbm, w_hbm, tg_hbm, neg_hbm, own_hbm, item_hbm,
    rows_out, numbers_out,
    ev_ref, w_ref, tg_ref, own_ref, item_ref,
    negs, mixes, poss, ids_send, ids_recv, rows_send, rows_recv,
    state_own, state_in, state_mid, state_mid_in,
    adj_own, adj_in, adj_mid, adj_mid_in,
    acc,
    sem_local, sem_ids, sem_near, sem_far, sem_cross, sem_pass, sem_mix, sem_pos,
    sem_st, sem_st2, sem_ad, sem_ad2, sem_rows,
):
    outer, inner = split_ctx(n_ctx)
    length, size = ev_hbm.shape
    neg_count = neg_hbm.shape[0]
    scale = 1.0 / math.sqrt(size * n_head)
    pairs = n_head // 2
    me = lax.axis_index("ctx")
    a, b = me // inner, me % inner
    h = lax.axis_index("head")
    p, c = h // 2, h % 2
    mate = p * 2 + (1 - c)

    barrier = pltpu.get_barrier_semaphore()

    def greet_ctx(k):
        pl.semaphore_signal(
            barrier, inc=1, device_id={"ctx": (me + k) % n_ctx}, device_id_type=MESH
        )

    def greet_head(k):
        pl.semaphore_signal(
            barrier, inc=1, device_id={"head": (h + k) % n_head}, device_id_type=MESH
        )

    times(n_ctx, greet_ctx)
    times(n_head, greet_head)

    def remote(src, dst, send, recv, **where):
        return pltpu.make_async_remote_copy(
            src_ref=src, dst_ref=dst, send_sem=send, recv_sem=recv,
            device_id=where, device_id_type=MESH,
        )

    loads = [
        pltpu.make_async_copy(src, dst, sem_local.at[i])
        for i, (src, dst) in enumerate(
            (
                (ev_hbm, ev_ref),
                (w_hbm, w_ref),
                (own_hbm, own_ref),
                (item_hbm, item_ref),
                (tg_hbm, tg_ref),
                (neg_hbm, negs.at[h]),
            )
        )
    ]
    for load in loads:
        load.start()
    loads[0].wait()
    loads[1].wait()

    ev = ev_ref[...]
    raw_k = mm(ev, w_ref[1])
    val = mm(ev, w_ref[2])
    slope_k = jnp.exp(jnp.minimum(raw_k, 0.0))
    km = slope_k + jnp.maximum(raw_k, 0.0)
    own_rows = state_own.shape[0]
    line_pad = lax.broadcasted_iota(jnp.int32, (own_rows - size, size), 0)

    def pack(mat, row):
        tail = jnp.where(line_pad == 0, jnp.broadcast_to(row, line_pad.shape), 0.0)
        return jnp.concatenate([mat, tail], axis=0)

    own_state = pack(mm(km, val, 0, 0), jnp.sum(km, axis=0, keepdims=True))
    state_own[...] = own_state.astype(BF)

    pl.semaphore_wait(barrier, n_ctx - 1 + n_head - 1)

    chunks = (pl.ds(0, 64), pl.ds(64, own_rows - 64))

    def outer_copy(own, slots, sem, k, r, forward):
        to = a + k if forward else a - k
        rows = chunks[r]
        return remote(
            own.at[rows], slots.at[k, rows], sem.at[0, k, r], sem.at[1, k, r],
            ctx=to * inner + b,
        )

    def outer_there(k, forward):
        return a + k < outer if forward else a - k >= 0

    def outer_start(own, slots, sem, forward):
        for r in range(len(chunks)):

            def step(k):
                @pl.when(outer_there(k, forward))
                def _():
                    outer_copy(own, slots, sem, k, r, forward).start()

            times(outer, step)

    def outer_sum(own, slots, sem, r, forward):
        rows = chunks[r]
        acc[rows] = jnp.zeros((rows.size, size), F32)

        def step(k):
            @pl.when(outer_there(k, not forward))
            def _():
                outer_copy(own, slots, sem, k, r, not forward).wait_recv()
                acc[rows] += slots[k, rows].astype(F32)

        times(outer, step)

    def outer_end(own, slots, sem, forward):
        for r in range(len(chunks)):

            def step(k):
                @pl.when(outer_there(k, forward))
                def _():
                    outer_copy(own, slots, sem, k, r, forward).wait_send()

            times(outer, step)

    def inner_copy(mids, slots, sem, j, r):
        to = a * inner + (b + j) % inner
        rows = chunks[r]
        return remote(
            mids.at[j, rows], slots.at[j, rows], sem.at[0, j, r], sem.at[1, j, r], ctx=to
        )

    def inner_start(own_value, mids, slots, sem, r, forward):
        rows = chunks[r]
        mine = own_value[rows.start : rows.start + rows.size]

        def step(j):
            to = (b + j) % inner
            passed = b < to if forward else b > to
            mids[j, rows] = (acc[rows] + jnp.where(passed, mine, 0.0)).astype(BF)
            inner_copy(mids, slots, sem, j, r).start()

        times(inner, step)

    def inner_sum(mids, slots, sem):
        for r in range(len(chunks)):
            rows = chunks[r]

            def step(j):
                inner_copy(mids, slots, sem, j, r).wait()
                acc[rows] += slots[j, rows].astype(F32)

            times(inner, step)

    def scan_turn(own_value, own, slots, sem, mids, mid_slots, mid_sem, forward):
        for r in range(len(chunks)):
            outer_sum(own, slots, sem, r, forward)
            inner_start(own_value, mids, mid_slots, mid_sem, r, forward)

    outer_start(state_own, state_in, sem_st, True)

    parts = 2
    piece = neg_count // (2 * parts)
    half = me % 2
    partner = me + 1 - 2 * half

    def neg_rows(which, r):
        return pl.ds(pl.multiple_of((which * parts + r) * piece, 16), piece)

    def neg_slot(k):
        return ((p - k + pairs) % pairs) * 2 + c

    def neg_near():
        return remote(neg_hbm, negs.at[h], sem_near.at[0], sem_near.at[1], head=mate)

    def neg_far(k, r):
        rows = neg_rows(half, r)
        to = ((p + k) % pairs) * 2 + c
        return remote(
            neg_hbm.at[rows], negs.at[h, rows],
            sem_far.at[0, k, r], sem_far.at[1, k, r], head=to,
        )

    def neg_from_far(k, r):
        block = negs.at[neg_slot(k), neg_rows(half, r)]
        return remote(block, block, sem_far.at[0, k, r], sem_far.at[1, k, r], head=neg_slot(k))

    def neg_cross(k, r):
        block = negs.at[neg_slot(k), neg_rows(half, r)]
        return remote(block, block, sem_cross.at[0, k, r], sem_cross.at[1, k, r], ctx=partner)

    def neg_from_cross(k, r):
        block = negs.at[neg_slot(k), neg_rows(1 - half, r)]
        return remote(block, block, sem_cross.at[0, k, r], sem_cross.at[1, k, r], ctx=partner)

    def neg_pass(k, r, turn):
        block = negs.at[neg_slot(k), neg_rows(half if turn == 0 else 1 - half, r)]
        return remote(
            block, block, sem_pass.at[0, k, r, turn], sem_pass.at[1, k, r, turn], head=mate
        )

    def neg_forward(r):
        for k in range(1, pairs):
            neg_from_far(k, r).wait_recv()
            neg_cross(k, r).start()
            neg_pass(k, r, 0).start()

    def neg_forward_cross(r):
        for k in range(1, pairs):
            neg_from_cross(k, r).wait_recv()
            neg_pass(k, r, 1).start()

    for r in range(parts):
        for k in range(1, pairs):
            neg_far(k, r).start()
    neg_near().start()

    raw_q = mm(ev, w_ref[0])
    slope_q = jnp.exp(jnp.minimum(raw_q, 0.0))
    qm = slope_q + jnp.maximum(raw_q, 0.0)
    at_row = lax.broadcasted_iota(jnp.int32, (length, length), 0)
    at_col = lax.broadcasted_iota(jnp.int32, (length, length), 1)
    causal = at_row >= at_col
    scores = jnp.where(causal, mm(qm, km, 1, 1), 0.0)
    scores_b = scores.astype(BF)
    numer = mm(scores_b, val)
    denom = jnp.sum(scores, axis=1, keepdims=True)

    scan_turn(own_state, state_own, state_in, sem_st, state_mid, state_mid_in, sem_st2, True)

    lanes = ids_send.shape[2]
    loads[2].wait()
    loads[3].wait()
    owner_row = own_ref[...]
    hot = (owner_row == lax.broadcasted_iota(jnp.int32, (lanes, length), 0)).astype(F32)
    earlier = mm(hot, (at_row < at_col).astype(F32))
    rank = jnp.sum(earlier * hot, axis=0, keepdims=True).astype(jnp.int32)
    rank_hot = (rank == lax.broadcasted_iota(jnp.int32, (lanes, length), 0)).astype(F32)
    number = item_ref[...] + 1
    high = mm(hot * (number // 16).astype(F32), rank_hot, 1, 1)
    low = mm(hot * (number % 16).astype(F32), rank_hot, 1, 1)
    numbers = (high * 16.0 + low).astype(jnp.int32)
    for d in range(n_ctx):
        ids_send[d] = numbers[d : d + 1, :]

    def ids_copy(k):
        to = (me + k) % n_ctx
        return remote(
            ids_send.at[to], ids_recv.at[me], sem_ids.at[0, k], sem_ids.at[1, k], ctx=to
        )

    def ids_from(k):
        at = (me - k + n_ctx) % n_ctx
        return remote(
            ids_send.at[at], ids_recv.at[at], sem_ids.at[0, k], sem_ids.at[1, k], ctx=at
        )

    times(n_ctx, lambda k: ids_copy(k).start())
    ids_recv[me] = ids_send[me]
    slot = owner_row * capacity + rank
    placing = (
        slot == lax.broadcasted_iota(jnp.int32, (n_ctx * capacity, length), 0)
    ).astype(F32).astype(BF)

    neg_forward(0)
    inner_sum(state_mid, state_mid_in, sem_st2)
    for r in range(1, parts):
        neg_forward(r)
    state = acc[0:size, :]
    total = acc[size : size + 1, :]
    state_b = state.astype(BF)

    numer = numer + mm(qm, state_b)
    denom = denom + jnp.sum(qm * total, axis=1, keepdims=True)
    inverse = 1.0 / denom
    att = numer * inverse
    mixed = (ev.astype(F32) + att).astype(BF)
    mixes[h] = mixed

    def mix_copy(k):
        to = (h + k) % n_head
        return remote(mixes.at[h], mixes.at[h], sem_mix.at[0, k], sem_mix.at[1, k], head=to)

    def mix_from(k):
        at = (h - k + n_head) % n_head
        return remote(mixes.at[at], mixes.at[at], sem_mix.at[0, k], sem_mix.at[1, k], head=at)

    def pos_copy(k):
        to = (h + k) % n_head
        return remote(poss.at[h], poss.at[h], sem_pos.at[0, k], sem_pos.at[1, k], head=to)

    def pos_from(k):
        at = (h - k + n_head) % n_head
        return remote(poss.at[at], poss.at[at], sem_pos.at[0, k], sem_pos.at[1, k], head=at)

    for k in range(1, n_head):
        mix_copy(k).start()
    loads[4].wait()
    targets = tg_ref[...].astype(F32)
    pos = jnp.sum(mixed.astype(F32) * targets, axis=1, keepdims=True)
    poss[h] = jnp.broadcast_to(pos, (length, size)).T[0:8, :]
    for k in range(1, n_head):
        pos_copy(k).start()

    for r in range(parts):
        neg_forward_cross(r)
    for k in range(1, n_head):
        mix_from(k).wait_recv()
        pos_from(k).wait_recv()
    loads[5].wait()
    neg_near().wait_recv()
    for k in range(1, pairs):
        for r in range(parts):
            neg_pass(k, r, 0).wait_recv()
            neg_pass(k, r, 1).wait_recv()

    pos_all = poss[0]
    for k in range(1, n_head):
        pos_all = pos_all + poss[k]
    pos_col = pos_all.T[:, 0:1] * (0.5 * scale)
    mixed_all = jnp.concatenate([mixes[k] for k in range(n_head)], axis=1)

    grad = jnp.zeros((length, size), F32)
    coef = jnp.zeros((length, 1), F32)
    for i in range(pieces):
        rows = pl.ds(i * (neg_count // pieces), neg_count // pieces)
        block = jnp.concatenate([negs[k, rows] for k in range(n_head)], axis=1)
        score = mm(mixed_all, block, 1, 1)
        sigma = 0.5 + 0.5 * jnp.tanh(score * (0.5 * scale) - pos_col)
        coef = coef + jnp.sum(sigma, axis=1, keepdims=True)
        grad = grad + mm((sigma * (1.0 / neg_count)).astype(BF), negs[h, rows])
    grad = grad - (coef * (1.0 / neg_count)) * targets

    d_num = grad * inverse
    d_den = -jnp.sum(grad * att, axis=1, keepdims=True) * inverse
    d_num_b = d_num.astype(BF)
    qm_b = qm.astype(BF)
    own_adj = pack(mm(qm_b, d_num_b, 0, 0), jnp.sum(d_den * qm, axis=0, keepdims=True))
    adj_own[...] = own_adj.astype(BF)
    outer_start(adj_own, adj_in, sem_ad, False)

    weight = jnp.where(causal, mm(d_num_b, val, 1, 1) + d_den, 0.0).astype(BF)
    d_val = mm(scores_b, d_num_b, 0, 0)
    d_key = mm(weight, qm_b, 0, 0)
    d_query = mm(d_num_b, state_b, 1, 1) + d_den * total + mm(weight, km)
    grad = grad + mm(d_query * slope_q, w_ref[0], 1, 1)

    scan_turn(own_adj, adj_own, adj_in, sem_ad, adj_mid, adj_mid_in, sem_ad2, False)

    times(n_ctx, lambda k: ids_from(k).wait_recv())
    numbers = jnp.concatenate([ids_recv[s][:, 0:capacity] for s in range(n_ctx)], axis=1)
    numbers_out[...] = numbers

    inner_sum(adj_mid, adj_mid_in, sem_ad2)
    adj = acc[0:size, :].astype(BF)
    adj_total = acc[size : size + 1, :]
    d_val = d_val + mm(km, adj)
    d_key = d_key + mm(val, adj, 1, 1) + adj_total
    grad = grad + mm(d_key * slope_k, w_ref[1], 1, 1) + mm(d_val, w_ref[2], 1, 1)
    placed = mm(placing, grad.astype(BF)).astype(BF)
    rows_send[...] = placed.reshape(n_ctx, capacity, size)

    def rows_copy(k):
        to = (me + k) % n_ctx
        return remote(
            rows_send.at[to], rows_recv.at[me], sem_rows.at[0, k], sem_rows.at[1, k], ctx=to
        )

    def rows_from(k):
        at = (me - k + n_ctx) % n_ctx
        return remote(
            rows_send.at[at], rows_recv.at[at], sem_rows.at[0, k], sem_rows.at[1, k], ctx=at
        )

    times(n_ctx, lambda k: rows_copy(k).start())
    rows_recv[me] = rows_send[me]

    outer_end(state_own, state_in, sem_st, True)
    outer_end(adj_own, adj_in, sem_ad, False)
    times(n_ctx, lambda k: ids_copy(k).wait_send())
    for k in range(1, n_head):
        mix_copy(k).wait_send()
        pos_copy(k).wait_send()
    neg_near().wait_send()
    for k in range(1, pairs):
        for r in range(parts):
            neg_far(k, r).wait_send()
            neg_cross(k, r).wait_send()
            neg_pass(k, r, 0).wait_send()
            neg_pass(k, r, 1).wait_send()
    times(n_ctx, lambda k: rows_copy(k).wait_send())
    times(n_ctx, lambda k: rows_from(k).wait_recv())
    rows_out[...] = rows_recv[...].reshape(n_ctx * capacity, size)


def place_rows(rows_ref, numbers_ref, out_ref):
    count = out_ref.shape[0]
    first = pl.program_id(0) * count + 1
    line = lax.broadcasted_iota(jnp.int32, (count, rows_ref.shape[0]), 0) + first
    picking = (numbers_ref[...] == line).astype(F32).astype(BF)
    out_ref[...] = mm(picking, rows_ref[...])


def body(n_ctx, n_head, events, w_proj, targets, negatives, owners, item_rows):
    length, size = events.shape
    neg_count = negatives.shape[0]
    capacity = -(-(3 * length // (2 * n_ctx)) // 16) * 16
    outer, inner = split_ctx(n_ctx)
    pieces = 3
    packed = size + 16
    lanes = max(128, n_ctx)
    dma = pltpu.SemaphoreType.DMA
    vmem = pl.BlockSpec(memory_space=pltpu.VMEM)
    scans = [
        pltpu.VMEM((packed, size), BF),
        pltpu.VMEM((outer, packed, size), BF),
        pltpu.VMEM((max(inner, 2), packed, size), BF),
        pltpu.VMEM((max(inner, 2), packed, size), BF),
    ]
    rows, numbers = pl.pallas_call(
        functools.partial(kernel, n_ctx, n_head, capacity, pieces),
        out_shape=(
            jax.ShapeDtypeStruct((n_ctx * capacity, size), BF),
            jax.ShapeDtypeStruct((1, n_ctx * capacity), jnp.int32),
        ),
        in_specs=[pl.BlockSpec(memory_space=pltpu.HBM)] * 6,
        out_specs=(vmem, vmem),
        scratch_shapes=[
            pltpu.VMEM((length, size), BF),
            pltpu.VMEM(w_proj.shape, BF),
            pltpu.VMEM((length, size), BF),
            pltpu.VMEM((1, length), jnp.int32),
            pltpu.VMEM((1, length), jnp.int32),
            pltpu.VMEM((n_head, neg_count, size), BF),
            pltpu.VMEM((n_head, length, size), BF),
            pltpu.VMEM((n_head, 8, length), F32),
            pltpu.VMEM((n_ctx, 1, lanes), jnp.int32),
            pltpu.VMEM((n_ctx, 1, lanes), jnp.int32),
            pltpu.VMEM((n_ctx, capacity, size), BF),
            pltpu.VMEM((n_ctx, capacity, size), BF),
            *scans,
            *scans,
            pltpu.VMEM((packed, size), F32),
            dma((6,)),
            dma((2, n_ctx)),
            dma((2,)),
            dma((2, n_head // 2, 2)),
            dma((2, n_head // 2, 2)),
            dma((2, n_head // 2, 2, 2)),
            dma((2, n_head)),
            dma((2, n_head)),
            dma((2, outer, 2)),
            dma((2, max(inner, 2), 2)),
            dma((2, outer, 2)),
            dma((2, max(inner, 2), 2)),
            dma((2, n_ctx)),
        ],
        compiler_params=pltpu.CompilerParams(
            collective_id=0, has_side_effects=True, vmem_limit_bytes=56 * 1024 * 1024
        ),
    )(
        events,
        w_proj,
        targets,
        negatives,
        owners.reshape(1, length),
        item_rows.reshape(1, length),
    )
    blocks = 1
    return pl.pallas_call(
        place_rows,
        grid=(blocks,),
        out_shape=jax.ShapeDtypeStruct((ROWS_OWN, size), F32),
        in_specs=[
            pl.BlockSpec((n_ctx * capacity, size), lambda i: (0, 0)),
            pl.BlockSpec((1, n_ctx * capacity), lambda i: (0, 0)),
        ],
        out_specs=pl.BlockSpec((ROWS_OWN // blocks, size), lambda i: (i, 0)),
        compiler_params=pltpu.CompilerParams(vmem_limit_bytes=56 * 1024 * 1024),
    )(rows, numbers)


def solution(mesh):
    placed = (
        P("ctx", "head"),
        P(None, "head", None),
        P("ctx", "head"),
        P(None, "head"),
        P("ctx", None),
        P("ctx"),
    )
    return jax.shard_map(
        functools.partial(body, mesh.shape["ctx"], mesh.shape["head"]),
        mesh=mesh, in_specs=placed, out_specs=P("ctx", "head"), check_vma=False,
    )
```
